32 devices in a mesh: group: 4 (over x, core), slab: 8 (over z, y).
Axes of the slice: x: 2, y: 2, z: 4, core: 2. Of those that a mesh axis runs over, the one named last changes fastest.
Arguments:
- initial_samples: float32 [96, 64, 4096], P('group', 'slab'), may hold values from -6 to 6
- transport_ratios: float32 [3, 64, 4096], P(None, 'slab'), may hold values from 0.05 to 0.33
- assignment: int32 [96], replicated, may hold values from 0 to 95, each once
- obs_values: float32 [512, 512], P(('group', 'slab')), may hold values from -6 to 6
- obs_error: float32 [512, 512], P(('group', 'slab')), may hold values from 0.25 to 4
- sensor_easting_offset: int32 [512, 512], P(('group', 'slab')), may hold values from 0 to 63
- obs_column: int32 [512, 512], P(('group', 'slab')), may hold values from 0 to 23
- obs_count: int32 [512], P(('group', 'slab')), may hold values from 1 to 512, 131072 in all
Outputs:
- analysis: float32 [96, 64, 4096], P('group', 'slab')
The draws below stay inside these ranges and needn't reach their ends.
Inputs may be any that keep to these rules, and one draw needn't show every extreme that they name: `assignment`: a permutation of the members. A block's live observations are its first obs_count entries; some block has exactly 512.
All inputs are finite; a program needn't handle non-finite values.
Results may differ from the reference program's by a relative error of at most 0.0003.
Values sent between devices are 32-bit elements; how exact they have to be, the bound alone decides.
No kernel may reach another device: no remote copies, remote signals or barrier semaphores. Data moves between devices by JAX's collectives and lax.ppermute only.
A program may use at most 64 MiB of HBM per device.

```python
import math
import jax
import jax.numpy as jnp
import numpy as np
from jax import lax

MEMBERS = 96
NZ = 64
STEPS = 6
TILE_WIDTH = 8
HC = 8
OBS = 512
ITERS = 8
NX = 64
NYZ = 4096
NB = 512


def touch_ends(entries, key, low, high):
    extent = entries.shape
    index_at = [jax.random.randint(jax.random.fold_in(key, axis), (), 0, extent[axis]) for axis in range(len(extent))]
    entries = entries.at[tuple(index_at)].set(low)
    longest = extent.index(max(extent))
    index_at[longest] = (index_at[longest] + 1) % extent[longest]
    return entries.at[tuple(index_at)].set(high)


def block_levels(stream_key, shape, split, smallest, high):
    factor_of = 1.0
    for axis_at, shards_of in split:
        draws = jax.random.uniform(jax.random.fold_in(jax.random.fold_in(stream_key, 6), axis_at), (shards_of,), jnp.float32, smallest / len(split), high / len(split))
        factor_of = factor_of * jnp.repeat(jnp.exp(draws), shape[axis_at] // shards_of).reshape((-1,) + (1,) * (len(shape) - 1 - axis_at))
    return factor_of


def length_profile(count, total, bound, lean):
    loads = [(1 << 20) // math.isqrt(grade ** lean) + 1 for grade in range(2, count + 1)]
    spare, holding = total - bound - (count - 1), [1] * (count - 1)
    while spare > 0:
        candidates = [i for i in range(count - 1) if holding[i] < bound]
        mass, budget = sum([loads[i] for i in candidates]), spare
        for i in candidates:
            addition = min(bound - holding[i], max(1, budget * loads[i] // mass), spare)
            holding[i] = holding[i] + addition
            spare = spare - addition
    return np.array([bound] + holding)


def uneven(own_key, number_of, total, reach, slope):
    if number_of == 2:
        one = jax.random.randint(own_key, (), max(1, total - reach), min(reach, total - 1) + 1)
        return jnp.stack([one, total - one])
    tallies = jnp.asarray(length_profile(number_of, total, reach, slope), jnp.int32)
    pairs = (number_of - 1) // 2
    giver, receiver = tallies[1:1 + 2 * pairs:2], tallies[2:2 + 2 * pairs:2]
    slack = jnp.minimum(giver - 1, reach - receiver)
    passed = jax.random.randint(jax.random.fold_in(own_key, 1), (pairs,), 0, 1 << 20) % (slack + 1)
    tallies = tallies.at[1:1 + 2 * pairs:2].set(giver - passed).at[2:2 + 2 * pairs:2].set(receiver + passed)
    return tallies[jax.random.permutation(jax.random.fold_in(own_key, 2), number_of)]


def centred(key, extent, scale, reach, split=(), held_as=jnp.bfloat16):
    loudness = block_levels(key, extent, split, -0.22, 0.18) if split else 1.0
    array = jax.random.normal(key, extent, jnp.float32) * scale * loudness
    return jnp.minimum(jnp.maximum(array, -reach), reach).astype(held_as)


def setup_inputs(seed: int = 0) -> dict:
    streams_of = jax.random.split(jax.random.key(seed), 9)
    return {
        "initial_samples": centred(streams_of[0], (MEMBERS, NX, NYZ), 1.0, 6.0, ((0, 4), (1, 8)), jnp.float32),
        "transport_ratios": jnp.clip(0.05 + 0.28 * jax.random.uniform(streams_of[1], (3, NX, NYZ), jnp.float32) ** block_levels(streams_of[1], (3, NX, NYZ), ((1, 8),), -0.2, 0.2), 0.05, 0.33),
        "assignment": jax.random.permutation(streams_of[2], MEMBERS).astype(jnp.int32),
        "obs_values": centred(streams_of[3], (NB, OBS), 1.0, 6.0, ((0, 32),), jnp.float32),
        "obs_error": jnp.clip(jnp.exp(math.log(4.0) - 2.7725887 * jax.random.uniform(streams_of[4], (NB, OBS), jnp.float32) ** block_levels(streams_of[4], (NB, OBS), ((0, 32),), -0.2, 0.2)), 0.25, 4.0),
        "sensor_easting_offset": touch_ends(jax.random.randint(streams_of[5], (NB, OBS), 0, NX), jax.random.fold_in(streams_of[5], 1), 0, NX - 1).astype(jnp.int32),
        "obs_column": touch_ends(jax.random.randint(streams_of[6], (NB, OBS), 0, TILE_WIDTH + 2 * HC), jax.random.fold_in(streams_of[6], 1), 0, (TILE_WIDTH + 2 * HC) - 1).astype(jnp.int32),
        "obs_count": uneven(streams_of[7], NB, NB * OBS // 2, OBS, 2).astype(jnp.int32),
    }


def advance(sample_state, rates):
    z_position = jnp.arange(sample_state.shape[1]) % NZ
    upwind = jnp.roll(sample_state, 1, axis=0)
    below_y = jnp.roll(sample_state, NZ, axis=1)
    below_z = jnp.where(z_position == 0, jnp.roll(sample_state, 1 - NZ, axis=1), jnp.roll(sample_state, 1, axis=1))
    return sample_state - rates[0] * (sample_state - upwind) - rates[1] * (sample_state - below_y) - rates[2] * (sample_state - below_z)

def transport_sample_downstream(sample_state, transport_ratios):
    for section in range(STEPS):
        sample_state = advance(sample_state, transport_ratios)
    return sample_state

def reference(initial_samples, transport_ratios, assignment, obs_values, obs_error, sensor_easting_offset, obs_column, obs_count):
    hi = lax.Precision.HIGHEST
    prior_sample_set = lax.map(lambda sample_state: transport_sample_downstream(sample_state, transport_ratios), initial_samples)
    identity = jnp.eye(MEMBERS, dtype=jnp.float32)
    one_hot = (assignment[:, None] == jnp.arange(MEMBERS, dtype=jnp.int32)[None, :]).astype(jnp.float32)
    slots = jnp.arange(OBS, dtype=jnp.int32)

    def analyse(update_tile):
        vertical_line_positions = (TILE_WIDTH * update_tile - HC + obs_column[update_tile]) % NYZ
        modelled_readings = prior_sample_set[:, sensor_easting_offset[update_tile], vertical_line_positions]
        pred_mean = lax.optimization_barrier(jnp.mean(modelled_readings, axis=0))
        weight = jnp.where(slots < obs_count[update_tile], 1.0 / jnp.sqrt(obs_error[update_tile] * (MEMBERS - 1.0)), 0.0)
        scaled = (modelled_readings - pred_mean) * weight
        innovation = (obs_values[update_tile] - pred_mean) * weight
        gram = identity + jnp.dot(scaled, scaled.T, precision=hi)
        fro_norm = jnp.sqrt(jnp.sum(gram * gram))
        iterate_a = gram / fro_norm
        iterate_z = identity
        for iteration in range(ITERS):
            middle = 1.5 * identity - 0.5 * jnp.dot(iterate_z, iterate_a, precision=hi)
            iterate_a = jnp.dot(iterate_a, middle, precision=hi)
            iterate_z = jnp.dot(middle, iterate_z, precision=hi)
        transform = iterate_z / jnp.sqrt(fro_norm)
        projected = jnp.dot(scaled, innovation, precision=hi)
        mean_weights = jnp.dot(transform, jnp.dot(transform, projected, precision=hi), precision=hi)
        weights_all = mean_weights[:, None] + transform
        ordered = jnp.dot(weights_all, one_hot, precision=hi)
        mesh_volumes = lax.dynamic_slice_in_dim(prior_sample_set, (TILE_WIDTH * update_tile).astype(jnp.int32), TILE_WIDTH, 2)
        cell_mean = lax.optimization_barrier(jnp.mean(mesh_volumes, axis=0))
        return cell_mean[None] + jnp.einsum('mj,mxc->jxc', ordered, mesh_volumes - cell_mean[None], precision=hi)
    blocks = lax.map(analyse, jnp.arange(NB, dtype=jnp.int32))
    return jnp.transpose(blocks, (1, 2, 0, 3)).reshape(MEMBERS, NX, NYZ)
```

```python
import functools

import jax
import jax.numpy as jnp
from jax import lax
from jax.experimental import pallas as pl
from jax.experimental.pallas import tpu as pltpu
from jax.sharding import PartitionSpec as P

MEMBERS = 96
NZ = 64
STEPS = 6
TILE_WIDTH = 8
HC = 8
OBS = 512
ITERS = 8

LANES = 128
PLANES = 8
SPAN = 16
PACKED = 48
F32 = jnp.float32
BF16 = jnp.bfloat16
AXES = ("group", "slab")
VMEM = pl.BlockSpec(memory_space=pltpu.VMEM)
SMEM = pl.BlockSpec(memory_space=pltpu.SMEM)


def shifted(block, axis, distance):
    devices = range(lax.axis_size(axis))
    route = [((i - distance) % len(devices), i) for i in devices]
    return lax.ppermute(block, axis, route)


def lane_iota(rows=1):
    return lax.broadcasted_iota(jnp.int32, (rows, LANES), 1)


def split(x):
    high = x.astype(BF16)
    low = (x - high.astype(F32)).astype(BF16)
    return high, low


def dot(a, b, transposed=False):
    dims = (((1,), (1 if transposed else 0,)), ((), ()))
    return lax.dot_general(a, b, dims, preferred_element_type=F32)


def dot3(a, b, transposed=False):
    ah, al = a
    bh, bl = b
    return dot(ah, bh, transposed) + (dot(ah, bl, transposed) + dot(al, bh, transposed))


def dot3_deep(a, b):
    ah, al = a
    bh, bl = b
    return dot(jnp.concatenate([ah, al, ah], axis=1), jnp.concatenate([bh, bh, bl], axis=0))


def tile(j):
    return pl.ds(pl.multiple_of(j * LANES, LANES), LANES)


def plane_step(src, dst, slot, rates, plane, tiles):
    lane = lane_iota()
    z_first = (lane % NZ) == 0
    upper = lane >= NZ
    previous = src[slot, :, (tiles - 1) * LANES :]
    octets = src.shape[1] // 8
    for j in range(tiles):
        at = slice(j * LANES, (j + 1) * LANES)
        here = src[slot, :, at]
        upwind = src[slot - 1, :, at]
        below_y = pltpu.roll(jnp.where(upper, previous, here), NZ, 1)
        below_z = jnp.where(z_first, pltpu.roll(here, NZ + 1, 1), pltpu.roll(here, 1, 1))
        cx, cy, cz = (jnp.concatenate([rates[c, plane, :, at]] * octets, axis=0) for c in range(3))
        dst[slot, :, at] = here - cx * (here - upwind) - cy * (here - below_y) - cz * (here - below_z)
        previous = here


def fill(rates, wide):
    for c in range(3):
        for p in range(rates.shape[1]):
            wide[c, p] = jnp.broadcast_to(rates[c, p : p + 1, :], wide.shape[2:])


def first_kernel(x, ratios, skew, edge, a, b, rates):
    tiles = a.shape[2] // LANES
    fill(ratios, rates)

    def unpack(j, carry):
        a[:, :, tile(j)] = jnp.swapaxes(x[:, :, tile(j)], 0, 1)
        return carry

    lax.fori_loop(0, tiles, unpack, 0)
    edge[0] = a[PLANES - 1]

    def two_steps(kk, carry):
        k = 2 * kk + 1

        def up(i, c):
            plane_step(a, b, i, rates, i, tiles)
            return c

        def down(i, c):
            plane_step(b, a, i, rates, i, tiles)
            return c

        lax.fori_loop(k, PLANES, up, 0)
        edge[k] = b[PLANES - 1]
        lax.fori_loop(k + 1, PLANES, down, 0)

        @pl.when(k + 1 < STEPS)
        def _():
            edge[k + 1] = a[PLANES - 1]

        return carry

    lax.fori_loop(0, STEPS // 2, two_steps, 0)
    for p in range(PLANES):
        skew[p] = (a if min(p, STEPS) % 2 == 0 else b)[p]


def exchange_blocks(v):
    block = lane_iota() // SPAN
    for d in (4, 2, 1):
        high = (block // d) % 2 == 1
        out = list(v)
        for i in range(8):
            if (i // d) % 2 == 0:
                out[i] = jnp.where(high, pltpu.roll(v[i + d], SPAN * d, 1), v[i])
                out[i + d] = jnp.where(high, v[i + d], pltpu.roll(v[i], LANES - SPAN * d, 1))
        v = out
    return v


def second_kernel(half, slabs, skew, halo, ratios, zh, keep, send, a, b, rates):
    tiles = a.shape[2] // LANES
    fill(ratios, rates)
    for p in range(STEPS):
        (a if p % 2 == 0 else b)[p + 1] = skew[p]

    def two_steps(kk, carry):
        k = 2 * kk + 1

        def up(i, c):
            plane_step(a, b, i + 1, rates, i, tiles)
            return c

        def down(i, c):
            plane_step(b, a, i + 1, rates, i, tiles)
            return c

        a[0] = halo[k - 1]
        lax.fori_loop(0, k, up, 0)
        b[0] = halo[k]
        lax.fori_loop(0, k + 1, down, 0)
        return carry

    lax.fori_loop(0, STEPS // 2, two_steps, 0)

    lane = lane_iota()
    block = lane // SPAN

    def load(p, j):
        return a[p + 1, :, tile(j)] if p < STEPS else skew[p, :, tile(j)]

    def moved(p, j):
        before = lax.rem(j + (tiles - 1), tiles)
        return pltpu.roll(jnp.where(lane >= LANES - HC, load(p, before), load(p, j)), HC, 1)

    for out, which in ((send, 1 - zh[0]), (keep, zh[0])):

        def chunk(q, carry, out=out, which=which):
            j = lax.div(q, half) * slabs + which * half + lax.rem(q, half)
            groups = exchange_blocks([moved(p, j) for p in range(PLANES)])
            for t in range(8):
                out[q, :, t * LANES : (t + 1) * LANES] = groups[t]
            after = lax.rem(j + 1, tiles)
            last = moved(0, after)
            for p in range(1, PLANES):
                last = jnp.where(block == p, pltpu.roll(moved(p, after), SPAN * p, 1), last)
            out[q, :, 8 * LANES :] = last
            return carry

        lax.fori_loop(0, out.shape[0], chunk, 0)


def map_kernel(half, values, errors, x, column, count, zh, keep, send):
    rows = 4 * half
    row = lax.broadcasted_iota(jnp.int32, (rows, 1), 0)
    second = (row // (2 * half)) % 2
    slab = jnp.where(second == 1, 1 - zh[0], zh[0]) * half + row % half
    is_value = (row // half) % 2 == 1
    cell = lax.broadcasted_iota(jnp.int32, (2 * LANES, OBS), 0)
    slot = lax.broadcasted_iota(jnp.int32, (1, OBS), 1)

    def body(i, carry):
        place = column[i] + TILE_WIDTH * lax.rem(i, 2)
        xs = x[i]
        lanes = (place // SPAN) * LANES + (xs % PLANES) * SPAN + place % SPAN
        hits = jnp.where(cell == lanes, 1.0, 0.0).astype(BF16)
        squared = jnp.where(slot < count[i], 1.0 / (errors[i] * (MEMBERS - 1.0)), 0.0)
        entry = jnp.where(is_value, squared * values[i], squared)
        entry = jnp.where(xs // PLANES == slab, entry, 0.0)
        one, rest = split(entry)
        two, three = split(entry - one.astype(F32))
        sums = dot(jnp.concatenate([one, two, three], axis=0), hits, True)
        total = sums[:rows] + sums[rows : 2 * rows] + sums[2 * rows :]
        keep[i] = total[: 2 * half]
        send[i] = total[2 * half :]
        return carry

    lax.fori_loop(0, values.shape[0], body, 0)


def pack(m):
    lane = lane_iota()
    top = jnp.where(lane < 96, m[64:96], pltpu.roll(m[:32], 96, 1))
    low = jnp.where(lane < 64, m[32:48], pltpu.roll(m[48:64], 64, 1))
    return top, low


def unpack(top, low):
    lane = lane_iota()
    lower = jnp.concatenate(
        [
            jnp.where(lane < 32, pltpu.roll(top, 32, 1), 0.0),
            jnp.where(lane < 64, low, 0.0),
            jnp.where(lane < 64, pltpu.roll(low, 64, 1), 0.0),
            jnp.where(lane < 96, top, 0.0),
            jnp.zeros((32, LANES), F32),
        ],
        axis=0,
    )
    upper = lower.T
    row = lax.broadcasted_iota(jnp.int32, (LANES, LANES), 0)
    col = lax.broadcasted_iota(jnp.int32, (LANES, LANES), 1)
    return jnp.where(row // 32 >= col // 32, lower, upper)


def gram_kernel(half, fields, maps, out, anomaly, high, low, mean):
    groups, members = fields.shape[0] // half, fields.shape[1]
    blocks = maps.shape[0]
    for s in range(half):
        for t in range(fields.shape[2] // LANES):
            at = slice(t * LANES, (t + 1) * LANES)
            f = jnp.concatenate([fields[g * half + s, :, at] for g in range(groups)], axis=0)
            average = jnp.sum(f, axis=0, keepdims=True) / MEMBERS
            f = f - average
            mean[s, :, at] = average
            anomaly[s, :, at] = f
            fh, fl = split(f)
            high[s, :MEMBERS, at] = fh
            low[s, :MEMBERS, at] = fl
            high[s, MEMBERS:, at] = jnp.zeros((LANES - MEMBERS, LANES), BF16)
            low[s, MEMBERS:, at] = jnp.zeros((LANES - MEMBERS, LANES), BF16)

    def pair(i, carry):
        at = pl.ds(pl.multiple_of(i * LANES, LANES), 2 * LANES)
        total = None
        for s in range(half):
            f = anomaly[s, :, at]
            average = mean[s, :, at]
            parts, gammas = [], []
            for e in range(2):
                omega = maps[2 * i + e, s : s + 1, :]
                value = maps[2 * i + e, half + s : half + s + 1, :]
                parts.append(f * omega)
                gammas.append(value - omega * average)
            row = lax.broadcasted_iota(jnp.int32, (8, 2 * LANES), 0)
            extra = jnp.where(row == 0, gammas[0], jnp.where(row == 1, gammas[1], 0.0))
            left = split(jnp.concatenate(parts + [extra], axis=0))
            product = dot3(left, (high[s, :, at], low[s, :, at]), True)
            total = product if total is None else total + product
        for e in range(2):
            top, bottom = pack(total[e * MEMBERS : (e + 1) * MEMBERS])
            base = pl.multiple_of((2 * i + e) * PACKED, 8)
            out[pl.ds(base, 32), :] = top
            out[pl.ds(base + 32, 16), :] = bottom
            out[pl.ds(blocks * PACKED + 2 * i + e, 1), :] = total[2 * MEMBERS + e : 2 * MEMBERS + e + 1]
        return carry

    lax.fori_loop(0, blocks // 2, pair, 0)


def solve_kernel(batch, blocks, mine, other, out, left, right, scale):
    row = lax.broadcasted_iota(jnp.int32, (LANES, LANES), 0)
    col = lax.broadcasted_iota(jnp.int32, (LANES, LANES), 1)
    identity = jnp.where((row == col) & (row < MEMBERS), 1.0, 0.0)
    steps = blocks // batch

    def each(body):
        def several(j, carry):
            for e in range(batch):
                body(j * batch + e)
            return carry

        lax.fori_loop(0, steps, several, 0)

    def start(i):
        base = pl.multiple_of(i * PACKED, 8)
        top = mine[pl.ds(base, 32), :] + other[pl.ds(base, 32), :]
        low = mine[pl.ds(base + 32, 16), :] + other[pl.ds(base + 32, 16), :]
        g = identity + unpack(top, low)
        fro = jnp.sqrt(jnp.sum(jnp.sum(g * g, axis=0, keepdims=True), axis=1, keepdims=True))
        scale[i] = jnp.broadcast_to(fro, (8, LANES))
        left[i] = g * (1.0 / fro)

    def second(i):
        a = left[i]
        middle = 1.5 * identity - 0.5 * a
        left[i] = dot3(split(a), split(middle))
        right[i] = middle

    def iterate(i):
        aa, zz = split(left[i]), split(right[i])
        middle = split(1.5 * identity - 0.5 * dot3(zz, aa))
        left[i] = dot3(aa, middle)
        right[i] = dot3(middle, zz)

    def last(i):
        zz = split(right[i])
        middle = split(1.5 * identity - 0.5 * dot3(zz, split(left[i])))
        right[i] = dot3(middle, zz)

    def finish(i):
        transform = right[i, :MEMBERS] * (1.0 / jnp.sqrt(scale[i, :1]))
        at = pl.ds(blocks * PACKED + i, 1)
        inner = jnp.sum(transform * (mine[at, :] + other[at, :]), axis=1, keepdims=True)
        top, low = pack(transform)
        base = pl.multiple_of(i * PACKED, 8)
        out[pl.ds(base, 32), :] = top
        out[pl.ds(base + 32, 16), :] = low
        out[at, :] = jnp.sum(transform * inner, axis=0, keepdims=True)

    def loop(k, carry):
        each(iterate)
        return carry

    each(start)
    each(second)
    lax.fori_loop(1, ITERS - 1, loop, 0)
    each(last)
    each(finish)


def apply_kernel(half, blocks, fields, weights, assignment, out, result, planar):
    groups, members = fields.shape[0] // half, fields.shape[1]
    lane = lane_iota()
    first = (lane % SPAN) < TILE_WIDTH

    def pair(i, carry):
        sides = []
        for e in range(2):
            base = pl.multiple_of((2 * i + e) * PACKED, 8)
            t = unpack(weights[pl.ds(base, 32), :], weights[pl.ds(base + 32, 16), :])[:MEMBERS]
            sides.append(t + weights[pl.ds(blocks * PACKED + 2 * i + e, 1), :])
        left = split(jnp.concatenate(sides, axis=1))
        filler = jnp.zeros((LANES - MEMBERS, LANES), F32)
        for s in range(half):

            def rows(at):
                return jnp.concatenate([fields[g * half + s, :, at] for g in range(groups)], axis=0)

            x = jnp.where(
                first,
                pltpu.roll(rows(tile(i)), LANES - TILE_WIDTH, 1),
                pltpu.roll(rows(tile(i + 1)), TILE_WIDTH, 1),
            )
            average = jnp.sum(x, axis=0, keepdims=True) / MEMBERS
            x = x - average
            right = jnp.concatenate(
                [jnp.where(first, x, 0.0), filler, jnp.where(first, 0.0, x), filler], axis=0
            )
            result[s, i] = average + dot3(left, split(right))
        return carry

    lax.fori_loop(0, blocks // 2, pair, 0)
    for s in range(half):
        for r in range(MEMBERS // 8):
            at = slice(8 * r, 8 * r + 8)
            planes = exchange_blocks([result[s, i, at, :] for i in range(8)])
            for p in range(PLANES):
                planar[p * MEMBERS + 8 * r : p * MEMBERS + 8 * r + 8, :] = planes[p]

        def hand(n, carry, s=s):
            member = assignment[n]
            g, m = lax.div(member, members), lax.rem(member, members)
            out[g * half + s, m] = planar[pl.ds(n, PLANES, stride=MEMBERS), :]
            return carry

        lax.fori_loop(0, MEMBERS, hand, 0, unroll=8)


def join_kernel(half, mine, other, zh, out):
    for source, which in ((mine, zh[0]), (other, 1 - zh[0])):
        for s in range(half):
            out[:, :, tile(which * half + s)] = source[s]


def call(kernel, outs, scratch, *args, specs=None, cost=None):
    shapes = [jax.ShapeDtypeStruct(s, F32) for s in outs]
    return pl.pallas_call(
        kernel,
        out_shape=shapes if len(shapes) > 1 else shapes[0],
        in_specs=specs or [VMEM] * len(args),
        out_specs=[VMEM] * len(shapes) if len(shapes) > 1 else VMEM,
        scratch_shapes=scratch,
        compiler_params=pltpu.CompilerParams(vmem_limit_bytes=56 * 1024 * 1024),
        cost_estimate=cost,
    )(*args)


def work(flops, moved):
    return pl.CostEstimate(flops=flops, bytes_accessed=moved, transcendentals=0)


def planned(
    initial_samples,
    transport_ratios,
    assignment,
    obs_values,
    obs_error,
    sensor_easting_offset,
    obs_column,
    obs_count,
):
    members, planes, columns = initial_samples.shape
    slabs = lax.axis_size("slab")
    groups = lax.axis_size("group")
    half = slabs // 2
    peers = groups * half
    blocks = obs_values.shape[0]
    width = blocks // 2 * LANES + LANES
    zh = (lax.axis_index("slab") // half).astype(jnp.int32).reshape(1)
    teams = [
        [g * slabs + h * half + i for g in range(groups) for i in range(half)] for h in range(2)
    ]

    def spread(x):
        return lax.all_to_all(
            x, AXES, split_axis=0, concat_axis=0, tiled=True, axis_index_groups=teams
        )

    def partner(x):
        return shifted(x, "slab", half)

    whole = (planes, members, columns)
    wide = [pltpu.VMEM((3, planes, 8, columns), F32)]
    skew, edge = call(
        first_kernel,
        [whole, (STEPS, members, columns)],
        [pltpu.VMEM(whole, F32)] * 2 + wide,
        initial_samples,
        transport_ratios,
        cost=work(10**7, 10**7),
    )
    halo = shifted(edge, "slab", 1)
    map_shape = (blocks, 2 * half, 2 * LANES)
    map_keep, map_send = call(
        functools.partial(map_kernel, half),
        [map_shape, map_shape],
        [],
        *(x[:, None] for x in (obs_values, obs_error, sensor_easting_offset, obs_column)),
        obs_count,
        zh,
        specs=[VMEM] * 4 + [SMEM] * 2,
        cost=work(10**8, 10**6),
    )
    map_recv = partner(map_send)
    payload = (peers, members, width)
    keep, send = call(
        functools.partial(second_kernel, half, slabs),
        [payload, payload],
        [pltpu.VMEM((STEPS + 1, members, columns), F32)] * 2 + wide,
        skew,
        halo,
        transport_ratios,
        zh,
        specs=[VMEM] * 3 + [SMEM],
        cost=work(10**7, 10**7),
    )
    packed = (blocks * PACKED + blocks, LANES)

    def gram(fields, maps):
        return call(
            functools.partial(gram_kernel, half),
            [packed],
            [
                pltpu.VMEM((half, MEMBERS, width), F32),
                pltpu.VMEM((half, LANES, width), BF16),
                pltpu.VMEM((half, LANES, width), BF16),
                pltpu.VMEM((half, 1, width), F32),
            ],
            fields,
            maps,
            cost=work(10**9, 4 * 10**6),
        )

    def apply(fields, weights):
        return call(
            functools.partial(apply_kernel, half, blocks),
            [(peers, members, planes, LANES)],
            [
                pltpu.VMEM((half, blocks // 2, MEMBERS, LANES), F32),
                pltpu.VMEM((PLANES * MEMBERS, LANES), F32),
            ],
            fields,
            weights,
            assignment,
            specs=[VMEM] * 2 + [SMEM],
            cost=work(10**9, 4 * 10**6),
        )

    fields_send = spread(send)
    gram_other = partner(gram(fields_send, map_recv))
    fields_keep = spread(keep)
    gram_mine = gram(fields_keep, map_keep)
    weights = call(
        functools.partial(solve_kernel, 8, blocks),
        [packed],
        [pltpu.VMEM((blocks, LANES, LANES), F32)] * 2 + [pltpu.VMEM((blocks, 8, LANES), F32)],
        gram_mine,
        gram_other,
        cost=work(10**9, 10**6),
    )
    weights_other = partner(weights)
    result_mine = spread(apply(fields_keep, weights))
    result_other = spread(apply(fields_send, weights_other))
    part = pl.BlockSpec((half, members, planes, LANES), lambda g: (g, 0, 0, 0))
    return pl.pallas_call(
        functools.partial(join_kernel, half),
        out_shape=jax.ShapeDtypeStruct((members, planes, columns), F32),
        grid=(groups,),
        in_specs=[part, part, SMEM],
        out_specs=pl.BlockSpec((members, planes, slabs * LANES), lambda g: (0, 0, g)),
    )(result_mine, result_other, zh)


def padded(x, sides, width):
    for axis, dim in sides:
        size, length = (lax.axis_size(axis), x.shape[dim])
        up = [(i, (i + 1) % size) for i in range(size)]
        down = [(j, i) for i, j in up]
        last = lax.slice_in_dim(x, length - width, length, axis=dim)
        first = lax.slice_in_dim(x, 0, width, axis=dim)
        before = lax.ppermute(last, axis, up)
        after = lax.ppermute(first, axis, down)
        x = jnp.concatenate([before, x, after], axis=dim)
    return x


def advance(sample_state, upwind, rates):
    z_position = jnp.arange(sample_state.shape[2]) % NZ
    below_y = jnp.roll(sample_state, NZ, axis=2)
    below_z = jnp.where(
        z_position == 0, jnp.roll(sample_state, 1 - NZ, axis=2), jnp.roll(sample_state, 1, axis=2)
    )
    return (
        sample_state
        - rates[0] * (sample_state - upwind)
        - rates[1] * (sample_state - below_y)
        - rates[2] * (sample_state - below_z)
    )


def general(
    initial_samples,
    transport_ratios,
    assignment,
    obs_values,
    obs_error,
    sensor_easting_offset,
    obs_column,
    obs_count,
):
    hi = lax.Precision.HIGHEST
    local_members, planes, total_columns = initial_samples.shape
    group_count = lax.axis_size("group")
    slab_count = lax.axis_size("slab")
    own_columns = total_columns // (group_count * slab_count)
    state = initial_samples
    for section in range(STEPS):
        edge_plane = shifted(state[:, planes - 1 :], "slab", 1)
        upwind = jnp.concatenate([edge_plane, state[:, : planes - 1]], axis=1)
        state = advance(state, upwind, transport_ratios)
    pieces = lax.all_to_all(state, ("group", "slab"), split_axis=2, concat_axis=0, tiled=True)
    pieces = pieces.reshape(group_count, slab_count, local_members, planes, own_columns)
    vertical_line_positions = jnp.transpose(pieces, (0, 2, 1, 3, 4)).reshape(
        MEMBERS, slab_count * planes, own_columns
    )
    grid_x = vertical_line_positions.shape[1]
    own_blocks = obs_values.shape[0]
    block_start = (TILE_WIDTH * jnp.arange(own_blocks, dtype=jnp.int32))[:, None]
    edge_blocks = (HC + TILE_WIDTH - 1) // TILE_WIDTH
    window_col = block_start - HC + obs_column
    requests = jnp.stack([sensor_easting_offset, obs_column])
    asked = padded(requests, ((("group", "slab"), 1),), edge_blocks)
    left_asked = asked[:, :edge_blocks]
    right_asked = asked[:, edge_blocks + own_blocks :]
    edge_index = jnp.arange(edge_blocks, dtype=jnp.int32)[:, None]
    left_cols = (
        TILE_WIDTH * (own_blocks - edge_blocks + edge_index) - HC + left_asked[1] - own_columns
    )
    right_cols = TILE_WIDTH * edge_index - HC + right_asked[1] + own_columns
    serve_level = jnp.concatenate([left_asked[0], right_asked[0]], axis=0)
    serve_cols = jnp.clip(jnp.concatenate([left_cols, right_cols], axis=0), 0, own_columns - 1)
    flattened = vertical_line_positions.reshape(MEMBERS, grid_x * own_columns)
    serve_pos = (serve_level * own_columns + serve_cols).reshape(-1)
    served = jnp.take(flattened, serve_pos, axis=1).reshape(MEMBERS, 2 * edge_blocks, OBS)
    answered = padded(served, ((("group", "slab"), 1),), edge_blocks)
    from_left = answered[:, :edge_blocks]
    from_right = answered[:, 3 * edge_blocks :]
    filler = jnp.zeros((MEMBERS, own_blocks - edge_blocks, OBS), jnp.float32)
    left_full = jnp.concatenate([from_left, filler], axis=1)
    right_full = jnp.concatenate([filler, from_right], axis=1)
    local_pos = (
        sensor_easting_offset * own_columns + jnp.clip(window_col, 0, own_columns - 1)
    ).reshape(-1)
    local_vals = jnp.take(flattened, local_pos, axis=1).reshape(MEMBERS, own_blocks, OBS)
    modelled_readings = jnp.where(
        window_col[None] < 0,
        left_full,
        jnp.where(window_col[None] >= own_columns, right_full, local_vals),
    )
    slots = jnp.arange(OBS, dtype=jnp.int32)[None, :]
    pred_mean = jnp.mean(modelled_readings, axis=0)
    weight = jnp.where(slots < obs_count[:, None], 1.0 / jnp.sqrt(obs_error * (MEMBERS - 1.0)), 0.0)
    scaled = jnp.transpose((modelled_readings - pred_mean[None]) * weight[None], (1, 0, 2))
    innovation = (obs_values - pred_mean) * weight
    identity = jnp.eye(MEMBERS, dtype=jnp.float32)
    gram = identity[None] + jnp.einsum("bmk,bnk->bmn", scaled, scaled, precision=hi)
    fro_norm = jnp.sqrt(jnp.sum(gram * gram, axis=(1, 2)))
    iterate_a = gram / fro_norm[:, None, None]
    iterate_z = jnp.broadcast_to(identity, gram.shape)
    for iteration in range(ITERS):
        middle = 1.5 * identity[None] - 0.5 * jnp.einsum(
            "bij,bjk->bik", iterate_z, iterate_a, precision=hi
        )
        iterate_a = jnp.einsum("bij,bjk->bik", iterate_a, middle, precision=hi)
        iterate_z = jnp.einsum("bij,bjk->bik", middle, iterate_z, precision=hi)
    transform = iterate_z / jnp.sqrt(fro_norm)[:, None, None]
    projected = jnp.einsum("bmk,bk->bm", scaled, innovation, precision=hi)
    inner_step = jnp.einsum("bmn,bn->bm", transform, projected, precision=hi)
    mean_weights = jnp.einsum("bmn,bn->bm", transform, inner_step, precision=hi)
    weights_all = mean_weights[:, :, None] + transform
    one_hot = (assignment[:, None] == jnp.arange(MEMBERS, dtype=jnp.int32)[None, :]).astype(
        jnp.float32
    )
    ordered = jnp.einsum("bmn,nj->bmj", weights_all, one_hot, precision=hi)
    column_weights = jnp.repeat(ordered, TILE_WIDTH, axis=0)
    column_major = jnp.transpose(vertical_line_positions, (2, 0, 1))
    cell_mean = jnp.mean(column_major, axis=1)
    updated = cell_mean[:, None, :] + jnp.einsum(
        "cmj,cmx->cjx", column_weights, column_major - cell_mean[:, None, :], precision=hi
    )
    analysed = jnp.transpose(updated, (1, 2, 0))
    outgoing = analysed.reshape(group_count, local_members, slab_count, planes, own_columns)
    outgoing = jnp.transpose(outgoing, (0, 2, 1, 3, 4)).reshape(
        group_count * slab_count * local_members, planes, own_columns
    )
    result = lax.all_to_all(outgoing, ("group", "slab"), split_axis=0, concat_axis=2, tiled=True)
    return result


def shards(initial_samples, transport_ratios, assignment, obs_values, *rest):
    members, planes, columns = initial_samples.shape
    blocks = obs_values.shape[0]
    fits = (
        planes == PLANES
        and members % 8 == 0
        and blocks * TILE_WIDTH == LANES
        and lax.axis_size("slab") == 8
        and columns % LANES == 0
    )
    path = planned if fits else general
    return path(initial_samples, transport_ratios, assignment, obs_values, *rest)


def solution(mesh):
    placed = (
        P("group", "slab", None),
        P(None, "slab", None),
        P(),
        P(("group", "slab"), None),
        P(("group", "slab"), None),
        P(("group", "slab"), None),
        P(("group", "slab"), None),
        P(("group", "slab")),
    )
    return jax.shard_map(
        shards, mesh=mesh, in_specs=placed, out_specs=P("group", "slab", None), check_vma=False
    )
```

```python
import functools

import jax
import jax.numpy as jnp
from jax import lax
from jax.experimental import pallas as pl
from jax.experimental.pallas import tpu as pltpu
from jax.sharding import PartitionSpec as P


MEMBERS = 96
NZ = 64
STEPS = 6
TILE_WIDTH = 8
HC = 8
OBS = 512
ITERS = 8

LANES = 128
PLANES = 8
SPAN = 16
PACKED = 48
BATCH = 4
F32 = jnp.float32
BF16 = jnp.bfloat16
AXES = ("group", "slab")
VMEM = pl.BlockSpec(memory_space=pltpu.VMEM)
SMEM = pl.BlockSpec(memory_space=pltpu.SMEM)


def shifted(block, axis, distance):
    devices = range(lax.axis_size(axis))
    route = [((i - distance) % len(devices), i) for i in devices]
    return lax.ppermute(block, axis, route)


def lane_iota(rows=1):
    return lax.broadcasted_iota(jnp.int32, (rows, LANES), 1)


def split(x):
    high = x.astype(BF16)
    low = (x - high.astype(F32)).astype(BF16)
    return high, low


def dot(a, b, transposed=False):
    dims = (((1,), (1 if transposed else 0,)), ((), ()))
    return lax.dot_general(a, b, dims, preferred_element_type=F32)


def dot3(a, b, transposed=False):
    ah, al = a
    bh, bl = b
    return dot(ah, bh, transposed) + (dot(ah, bl, transposed) + dot(al, bh, transposed))


def tile(j):
    return pl.ds(pl.multiple_of(j * LANES, LANES), LANES)


def plane_step(src, dst, slot, rates, plane, tiles):
    lane = lane_iota()
    z_first = (lane % NZ) == 0
    upper = lane >= NZ
    octets = src.shape[1] // 8

    def at(j):
        j = (j + tiles) % tiles
        return slice(j * LANES, (j + 1) * LANES)

    for base in range(0, tiles, BATCH):
        these = range(base, min(base + BATCH, tiles))
        here = [src[slot, :, at(j)] for j in (base - 1, *these)]
        upwind = [src[slot - 1, :, at(j)] for j in these]
        below_y = [pltpu.roll(jnp.where(upper, x, y), NZ, 1) for x, y in zip(here, here[1:])]
        here = here[1:]
        one = [pltpu.roll(x, 1, 1) for x in here]
        wrapped = [pltpu.roll(x, NZ + 1, 1) for x in here]
        below_z = [jnp.where(z_first, x, y) for x, y in zip(wrapped, one)]
        for j, u, ux, uy, uz in zip(these, here, upwind, below_y, below_z):
            cx, cy, cz = (
                jnp.concatenate([rates[c, plane, :, at(j)]] * octets, axis=0) for c in range(3)
            )
            dst[slot, :, at(j)] = u - cx * (u - ux) - cy * (u - uy) - cz * (u - uz)


def fill(rates, wide):
    for c in range(3):
        for p in range(rates.shape[1]):
            wide[c, p] = jnp.broadcast_to(rates[c, p : p + 1, :], wide.shape[2:])


def first_kernel(x, ratios, skew, edge, a, b, rates):
    tiles = a.shape[2] // LANES
    fill(ratios, rates)

    def unpack(j, carry):
        a[:, :, tile(j)] = jnp.swapaxes(x[:, :, tile(j)], 0, 1)
        return carry

    lax.fori_loop(0, tiles, unpack, 0)
    edge[0] = a[PLANES - 1]

    def two_steps(kk, carry):
        k = 2 * kk + 1

        def up(i, c):
            plane_step(a, b, i, rates, i, tiles)
            return c

        def down(i, c):
            plane_step(b, a, i, rates, i, tiles)
            return c

        lax.fori_loop(k, PLANES, up, 0)
        edge[k] = b[PLANES - 1]
        lax.fori_loop(k + 1, PLANES, down, 0)

        @pl.when(k + 1 < STEPS)
        def _():
            edge[k + 1] = a[PLANES - 1]

        return carry

    lax.fori_loop(0, STEPS // 2, two_steps, 0)
    for p in range(PLANES):
        skew[p] = (a if min(p, STEPS) % 2 == 0 else b)[p]


def exchange_blocks(v):
    block = lane_iota() // SPAN
    for d in (4, 2, 1):
        high = (block // d) % 2 == 1
        out = list(v)
        for i in range(8):
            if (i // d) % 2 == 0:
                out[i] = jnp.where(high, pltpu.roll(v[i + d], SPAN * d, 1), v[i])
                out[i + d] = jnp.where(high, v[i + d], pltpu.roll(v[i], LANES - SPAN * d, 1))
        v = out
    return v


def second_kernel(half, slabs, skew, halo, ratios, zh, keep, send, a, b, rates):
    tiles = a.shape[2] // LANES
    fill(ratios, rates)
    for p in range(STEPS):
        (a if p % 2 == 0 else b)[p + 1] = skew[p]

    def two_steps(kk, carry):
        k = 2 * kk + 1

        def up(i, c):
            plane_step(a, b, i + 1, rates, i, tiles)
            return c

        def down(i, c):
            plane_step(b, a, i + 1, rates, i, tiles)
            return c

        a[0] = halo[k - 1]
        lax.fori_loop(0, k, up, 0)
        b[0] = halo[k]
        lax.fori_loop(0, k + 1, down, 0)
        return carry

    lax.fori_loop(0, STEPS // 2, two_steps, 0)

    lane = lane_iota()
    block = lane // SPAN

    def load(p, j):
        return a[p + 1, :, tile(j)] if p < STEPS else skew[p, :, tile(j)]

    def moved(p, j):
        before = lax.rem(j + (tiles - 1), tiles)
        return pltpu.roll(jnp.where(lane >= LANES - HC, load(p, before), load(p, j)), HC, 1)

    for out, which in ((send, 1 - zh[0]), (keep, zh[0])):

        def chunk(q, carry, out=out, which=which):
            j = lax.div(q, half) * slabs + which * half + lax.rem(q, half)
            groups = exchange_blocks([moved(p, j) for p in range(PLANES)])
            for t in range(8):
                out[q, :, t * LANES : (t + 1) * LANES] = groups[t]
            after = lax.rem(j + 1, tiles)
            last = moved(0, after)
            for p in range(1, PLANES):
                last = jnp.where(block == p, pltpu.roll(moved(p, after), SPAN * p, 1), last)
            out[q, :, 8 * LANES :] = last
            return carry

        lax.fori_loop(0, out.shape[0], chunk, 0)


def map_kernel(half, values, errors, x, column, count, zh, keep, send):
    rows = 4 * half
    row = lax.broadcasted_iota(jnp.int32, (rows, 1), 0)
    second = (row // (2 * half)) % 2
    slab = jnp.where(second == 1, 1 - zh[0], zh[0]) * half + row % half
    is_value = (row // half) % 2 == 1
    cell = lax.broadcasted_iota(jnp.int32, (2 * LANES, OBS), 0)
    slot = lax.broadcasted_iota(jnp.int32, (1, OBS), 1)

    def body(i, carry):
        place = column[i] + TILE_WIDTH * lax.rem(i, 2)
        xs = x[i]
        lanes = (place // SPAN) * LANES + (xs % PLANES) * SPAN + place % SPAN
        hits = jnp.where(cell == lanes, 1.0, 0.0).astype(BF16)
        squared = jnp.where(slot < count[i], 1.0 / (errors[i] * (MEMBERS - 1.0)), 0.0)
        entry = jnp.where(is_value, squared * values[i], squared)
        entry = jnp.where(xs // PLANES == slab, entry, 0.0)
        one, _ = split(entry)
        two, three = split(entry - one.astype(F32))
        sums = dot(jnp.concatenate([one, two, three], axis=0), hits, True)
        total = sums[:rows] + sums[rows : 2 * rows] + sums[2 * rows :]
        keep[i] = total[: 2 * half]
        send[i] = total[2 * half :]
        return carry

    lax.fori_loop(0, values.shape[0], body, 0)


def pack(m):
    lane = lane_iota()
    top = jnp.where(lane < 96, m[64:96], pltpu.roll(m[:32], 96, 1))
    low = jnp.where(lane < 64, m[32:48], pltpu.roll(m[48:64], 64, 1))
    return top, low


def every(function, *lists):
    return [function(*x) for x in zip(*lists)]


def lower_blocks(top, low):
    lane = lane_iota()
    return jnp.concatenate(
        [
            jnp.where(lane < 32, pltpu.roll(top, 32, 1), 0.0),
            jnp.where(lane < 64, low, 0.0),
            jnp.where(lane < 64, pltpu.roll(low, 64, 1), 0.0),
            jnp.where(lane < 96, top, 0.0),
            jnp.zeros((32, LANES), F32),
        ],
        axis=0,
    )


def unpack(tops, lows):
    row = lax.broadcasted_iota(jnp.int32, (LANES, LANES), 0)
    col = lax.broadcasted_iota(jnp.int32, (LANES, LANES), 1)
    lower = every(lower_blocks, tops, lows)
    upper = [x.T for x in lower]
    return [jnp.where(row // 32 >= col // 32, x, y) for x, y in zip(lower, upper)]


def gram_kernel(half, fields, maps, out, anomaly, high, low, mean):
    groups = fields.shape[0] // half
    blocks = maps.shape[0]
    for s in range(half):
        for t in range(fields.shape[2] // LANES):
            at = slice(t * LANES, (t + 1) * LANES)
            f = jnp.concatenate([fields[g * half + s, :, at] for g in range(groups)], axis=0)
            average = jnp.sum(f, axis=0, keepdims=True) / MEMBERS
            f = f - average
            mean[s, :, at] = average
            anomaly[s, :, at] = f
            fh, fl = split(f)
            high[s, :MEMBERS, at] = fh
            low[s, :MEMBERS, at] = fl
            high[s, MEMBERS:, at] = jnp.zeros((LANES - MEMBERS, LANES), BF16)
            low[s, MEMBERS:, at] = jnp.zeros((LANES - MEMBERS, LANES), BF16)

    def pair(i, carry):
        at = pl.ds(pl.multiple_of(i * LANES, LANES), 2 * LANES)
        total = None
        for s in range(half):
            f = anomaly[s, :, at]
            average = mean[s, :, at]
            parts, gammas = [], []
            for e in range(2):
                omega = maps[2 * i + e, s : s + 1, :]
                value = maps[2 * i + e, half + s : half + s + 1, :]
                parts.append(f * omega)
                gammas.append(value - omega * average)
            row = lax.broadcasted_iota(jnp.int32, (8, 2 * LANES), 0)
            extra = jnp.where(row == 0, gammas[0], jnp.where(row == 1, gammas[1], 0.0))
            left = split(jnp.concatenate(parts + [extra], axis=0))
            product = dot3(left, (high[s, :, at], low[s, :, at]), True)
            total = product if total is None else total + product
        for e in range(2):
            top, bottom = pack(total[e * MEMBERS : (e + 1) * MEMBERS])
            base = pl.multiple_of((2 * i + e) * PACKED, 8)
            out[pl.ds(base, 32), :] = top
            out[pl.ds(base + 32, 16), :] = bottom
            out[pl.ds(blocks * PACKED + 2 * i + e, 1), :] = total[2 * MEMBERS + e : 2 * MEMBERS + e + 1]
        return carry

    lax.fori_loop(0, blocks // 2, pair, 0)


def solve_kernel(batch, blocks, mine, other, out, left, right, scale):
    row = lax.broadcasted_iota(jnp.int32, (LANES, LANES), 0)
    col = lax.broadcasted_iota(jnp.int32, (LANES, LANES), 1)
    identity = jnp.where((row == col) & (row < MEMBERS), 1.0, 0.0)
    steps = blocks // batch

    def each(body):
        def several(j, carry):
            at = [j * batch + e for e in range(batch)]
            for i, (a, z) in zip(at, body(at)):
                if a is not None:
                    left[i] = a
                if z is not None:
                    right[i] = z
            return carry

        lax.fori_loop(0, steps, several, 0)

    def middle(p):
        return split(1.5 * identity - 0.5 * p)

    def start(at):
        bases = [pl.multiple_of(i * PACKED, 8) for i in at]
        tops = [mine[pl.ds(x, 32), :] + other[pl.ds(x, 32), :] for x in bases]
        lows = [mine[pl.ds(x + 32, 16), :] + other[pl.ds(x + 32, 16), :] for x in bases]
        grams = [identity + x for x in unpack(tops, lows)]
        sums = [jnp.sum(g * g, axis=0, keepdims=True) for g in grams]
        sums = [jnp.sum(x, axis=1, keepdims=True) for x in sums]
        roots = [lax.rsqrt(x) for x in sums]
        for i, x in zip(at, roots):
            scale[i] = jnp.broadcast_to(x, (8, LANES))
        return [(g * x, None) for g, x in zip(grams, roots)]

    def second(at):
        a = [left[i] for i in at]
        m = [1.5 * identity - 0.5 * x for x in a]
        return zip(every(dot3, every(split, a), every(split, m)), m)

    def iterate(at):
        a = [split(left[i]) for i in at]
        z = [split(right[i]) for i in at]
        m = every(middle, every(dot3, z, a))
        return zip(every(dot3, a, m), every(dot3, m, z))

    def last(at):
        a = [split(left[i]) for i in at]
        z = [split(right[i]) for i in at]
        m = every(middle, every(dot3, z, a))
        return [(None, x) for x in every(dot3, m, z)]

    def finish(at):
        rows = [pl.ds(blocks * PACKED + i, 1) for i in at]
        done = [right[i, :MEMBERS] * jnp.sqrt(scale[i, :1]) for i in at]
        vectors = [mine[x, :] + other[x, :] for x in rows]
        inner = [jnp.sum(t * x, axis=1, keepdims=True) for t, x in zip(done, vectors)]
        means = [jnp.sum(t * x, axis=0, keepdims=True) for t, x in zip(done, inner)]
        packs = every(pack, done)
        for i, x, m, (top, low) in zip(at, rows, means, packs):
            base = pl.multiple_of(i * PACKED, 8)
            out[pl.ds(base, 32), :] = top
            out[pl.ds(base + 32, 16), :] = low
            out[x, :] = m
        return []

    def loop(k, carry):
        each(iterate)
        return carry

    each(start)
    each(second)
    lax.fori_loop(1, ITERS - 1, loop, 0)
    each(last)
    each(finish)


def apply_kernel(half, blocks, fields, weights, assignment, out, result, planar):
    groups, members = fields.shape[0] // half, fields.shape[1]
    lane = lane_iota()
    first = (lane % SPAN) < TILE_WIDTH

    def pair(i, carry):
        bases = [pl.multiple_of((2 * i + e) * PACKED, 8) for e in range(2)]
        tops = [weights[pl.ds(x, 32), :] for x in bases]
        sides = unpack(tops, [weights[pl.ds(x + 32, 16), :] for x in bases])
        rows_at = [pl.ds(blocks * PACKED + 2 * i + e, 1) for e in range(2)]
        sides = [t[:MEMBERS] + weights[x, :] for t, x in zip(sides, rows_at)]
        left = split(jnp.concatenate(sides, axis=1))
        filler = jnp.zeros((LANES - MEMBERS, LANES), F32)
        for s in range(half):

            def rows(at):
                return jnp.concatenate([fields[g * half + s, :, at] for g in range(groups)], axis=0)

            x = jnp.where(
                first,
                pltpu.roll(rows(tile(i)), LANES - TILE_WIDTH, 1),
                pltpu.roll(rows(tile(i + 1)), TILE_WIDTH, 1),
            )
            average = jnp.sum(x, axis=0, keepdims=True) / MEMBERS
            x = x - average
            right = jnp.concatenate(
                [jnp.where(first, x, 0.0), filler, jnp.where(first, 0.0, x), filler], axis=0
            )
            result[s, i] = average + dot3(left, split(right))
        return carry

    lax.fori_loop(0, blocks // 2, pair, 0)
    for s in range(half):
        for r in range(MEMBERS // 8):
            at = slice(8 * r, 8 * r + 8)
            planes = exchange_blocks([result[s, i, at, :] for i in range(8)])
            for p in range(PLANES):
                planar[p * MEMBERS + 8 * r : p * MEMBERS + 8 * r + 8, :] = planes[p]

        def hand(n, carry, s=s):
            member = assignment[n]
            g, m = lax.div(member, members), lax.rem(member, members)
            out[g * half + s, m] = planar[pl.ds(n, PLANES, stride=MEMBERS), :]
            return carry

        lax.fori_loop(0, MEMBERS, hand, 0, unroll=8)


def join_kernel(half, mine, other, zh, out):
    for source, which in ((mine, zh[0]), (other, 1 - zh[0])):
        for s in range(half):
            out[:, :, tile(which * half + s)] = source[s]


def call(kernel, outs, scratch, *args, specs=None, cost=None, room=20):
    shapes = [jax.ShapeDtypeStruct(s, F32) for s in outs]
    return pl.pallas_call(
        kernel,
        out_shape=shapes if len(shapes) > 1 else shapes[0],
        in_specs=specs or [VMEM] * len(args),
        out_specs=[VMEM] * len(shapes) if len(shapes) > 1 else VMEM,
        scratch_shapes=scratch,
        compiler_params=pltpu.CompilerParams(vmem_limit_bytes=room * 1024 * 1024),
        cost_estimate=cost,
    )(*args)


def work(flops, moved):
    return pl.CostEstimate(flops=flops, bytes_accessed=moved, transcendentals=0)


def planned(
    initial_samples,
    transport_ratios,
    assignment,
    obs_values,
    obs_error,
    sensor_easting_offset,
    obs_column,
    obs_count,
):
    members, planes, columns = initial_samples.shape
    slabs = lax.axis_size("slab")
    groups = lax.axis_size("group")
    half = slabs // 2
    peers = groups * half
    blocks = obs_values.shape[0]
    width = blocks // 2 * LANES + LANES
    zh = (lax.axis_index("slab") // half).astype(jnp.int32).reshape(1)
    teams = [
        [g * slabs + h * half + i for g in range(groups) for i in range(half)] for h in range(2)
    ]

    def spread(x):
        return lax.all_to_all(
            x, AXES, split_axis=0, concat_axis=0, tiled=True, axis_index_groups=teams
        )

    def partner(x):
        return shifted(x, "slab", half)

    whole = (planes, members, columns)
    wide = [pltpu.VMEM((3, planes, 8, columns), F32)]
    skew, edge = call(
        first_kernel,
        [whole, (STEPS, members, columns)],
        [pltpu.VMEM(whole, F32)] * 2 + wide,
        initial_samples,
        transport_ratios,
        cost=work(10**7, 10**7),
        room=22,
    )
    halo = shifted(edge, "slab", 1)
    map_shape = (blocks, 2 * half, 2 * LANES)
    map_keep, map_send = call(
        functools.partial(map_kernel, half),
        [map_shape, map_shape],
        [],
        *(x[:, None] for x in (obs_values, obs_error, sensor_easting_offset, obs_column)),
        obs_count,
        zh,
        specs=[VMEM] * 4 + [SMEM] * 2,
        cost=work(10**8, 10**6),
    )
    map_recv = partner(map_send)
    payload = (peers, members, width)
    keep, send = call(
        functools.partial(second_kernel, half, slabs),
        [payload, payload],
        [pltpu.VMEM((STEPS + 1, members, columns), F32)] * 2 + wide,
        skew,
        halo,
        transport_ratios,
        zh,
        specs=[VMEM] * 3 + [SMEM],
        cost=work(10**7, 10**7),
        room=22,
    )
    packed = (blocks * PACKED + blocks, LANES)

    def gram(fields, maps):
        return call(
            functools.partial(gram_kernel, half),
            [packed],
            [
                pltpu.VMEM((half, MEMBERS, width), F32),
                pltpu.VMEM((half, LANES, width), BF16),
                pltpu.VMEM((half, LANES, width), BF16),
                pltpu.VMEM((half, 1, width), F32),
            ],
            fields,
            maps,
            cost=work(10**9, 4 * 10**6),
        )

    def apply(fields, weights):
        return call(
            functools.partial(apply_kernel, half, blocks),
            [(peers, members, planes, LANES)],
            [
                pltpu.VMEM((half, blocks // 2, MEMBERS, LANES), F32),
                pltpu.VMEM((PLANES * MEMBERS, LANES), F32),
            ],
            fields,
            weights,
            assignment,
            specs=[VMEM] * 2 + [SMEM],
            cost=work(10**9, 4 * 10**6),
        )

    fields_send = spread(send)
    gram_send = gram(fields_send, map_recv)
    gram_other = partner(gram_send)
    fields_keep = spread(keep)
    gram_mine = gram(fields_keep, map_keep)
    weights = call(
        functools.partial(solve_kernel, blocks, blocks),
        [packed],
        [pltpu.VMEM((blocks, LANES, LANES), F32)] * 2 + [pltpu.VMEM((blocks, 8, LANES), F32)],
        gram_mine,
        gram_other,
        cost=work(10**9, 10**6),
    )
    weights_other = partner(weights)
    applied = apply(fields_keep, weights)
    result_mine = spread(applied)
    result_other = spread(apply(fields_send, weights_other))
    part = pl.BlockSpec((half, members, planes, LANES), lambda g: (g, 0, 0, 0))
    return pl.pallas_call(
        functools.partial(join_kernel, half),
        out_shape=jax.ShapeDtypeStruct((members, planes, columns), F32),
        grid=(groups,),
        in_specs=[part, part, SMEM],
        out_specs=pl.BlockSpec((members, planes, slabs * LANES), lambda g: (0, 0, g)),
    )(result_mine, result_other, zh)


def padded(x, sides, width):
    for axis, dim in sides:
        size, length = (lax.axis_size(axis), x.shape[dim])
        up = [(i, (i + 1) % size) for i in range(size)]
        down = [(j, i) for i, j in up]
        last = lax.slice_in_dim(x, length - width, length, axis=dim)
        first = lax.slice_in_dim(x, 0, width, axis=dim)
        before = lax.ppermute(last, axis, up)
        after = lax.ppermute(first, axis, down)
        x = jnp.concatenate([before, x, after], axis=dim)
    return x


def advance(sample_state, upwind, rates):
    z_position = jnp.arange(sample_state.shape[2]) % NZ
    below_y = jnp.roll(sample_state, NZ, axis=2)
    below_z = jnp.where(
        z_position == 0, jnp.roll(sample_state, 1 - NZ, axis=2), jnp.roll(sample_state, 1, axis=2)
    )
    return (
        sample_state
        - rates[0] * (sample_state - upwind)
        - rates[1] * (sample_state - below_y)
        - rates[2] * (sample_state - below_z)
    )


def general(
    initial_samples,
    transport_ratios,
    assignment,
    obs_values,
    obs_error,
    sensor_easting_offset,
    obs_column,
    obs_count,
):
    hi = lax.Precision.HIGHEST
    local_members, planes, total_columns = initial_samples.shape
    group_count = lax.axis_size("group")
    slab_count = lax.axis_size("slab")
    own_columns = total_columns // (group_count * slab_count)
    state = initial_samples
    for _ in range(STEPS):
        edge_plane = shifted(state[:, planes - 1 :], "slab", 1)
        upwind = jnp.concatenate([edge_plane, state[:, : planes - 1]], axis=1)
        state = advance(state, upwind, transport_ratios)
    pieces = lax.all_to_all(state, ("group", "slab"), split_axis=2, concat_axis=0, tiled=True)
    pieces = pieces.reshape(group_count, slab_count, local_members, planes, own_columns)
    vertical_line_positions = jnp.transpose(pieces, (0, 2, 1, 3, 4)).reshape(
        MEMBERS, slab_count * planes, own_columns
    )
    grid_x = vertical_line_positions.shape[1]
    own_blocks = obs_values.shape[0]
    block_start = (TILE_WIDTH * jnp.arange(own_blocks, dtype=jnp.int32))[:, None]
    edge_blocks = (HC + TILE_WIDTH - 1) // TILE_WIDTH
    window_col = block_start - HC + obs_column
    requests = jnp.stack([sensor_easting_offset, obs_column])
    asked = padded(requests, ((("group", "slab"), 1),), edge_blocks)
    left_asked = asked[:, :edge_blocks]
    right_asked = asked[:, edge_blocks + own_blocks :]
    edge_index = jnp.arange(edge_blocks, dtype=jnp.int32)[:, None]
    left_cols = (
        TILE_WIDTH * (own_blocks - edge_blocks + edge_index) - HC + left_asked[1] - own_columns
    )
    right_cols = TILE_WIDTH * edge_index - HC + right_asked[1] + own_columns
    serve_level = jnp.concatenate([left_asked[0], right_asked[0]], axis=0)
    serve_cols = jnp.clip(jnp.concatenate([left_cols, right_cols], axis=0), 0, own_columns - 1)
    flattened = vertical_line_positions.reshape(MEMBERS, grid_x * own_columns)
    serve_pos = (serve_level * own_columns + serve_cols).reshape(-1)
    served = jnp.take(flattened, serve_pos, axis=1).reshape(MEMBERS, 2 * edge_blocks, OBS)
    answered = padded(served, ((("group", "slab"), 1),), edge_blocks)
    from_left = answered[:, :edge_blocks]
    from_right = answered[:, 3 * edge_blocks :]
    filler = jnp.zeros((MEMBERS, own_blocks - edge_blocks, OBS), jnp.float32)
    left_full = jnp.concatenate([from_left, filler], axis=1)
    right_full = jnp.concatenate([filler, from_right], axis=1)
    local_pos = (
        sensor_easting_offset * own_columns + jnp.clip(window_col, 0, own_columns - 1)
    ).reshape(-1)
    local_vals = jnp.take(flattened, local_pos, axis=1).reshape(MEMBERS, own_blocks, OBS)
    modelled_readings = jnp.where(
        window_col[None] < 0,
        left_full,
        jnp.where(window_col[None] >= own_columns, right_full, local_vals),
    )
    slots = jnp.arange(OBS, dtype=jnp.int32)[None, :]
    pred_mean = jnp.mean(modelled_readings, axis=0)
    weight = jnp.where(slots < obs_count[:, None], 1.0 / jnp.sqrt(obs_error * (MEMBERS - 1.0)), 0.0)
    scaled = jnp.transpose((modelled_readings - pred_mean[None]) * weight[None], (1, 0, 2))
    innovation = (obs_values - pred_mean) * weight
    identity = jnp.eye(MEMBERS, dtype=jnp.float32)
    gram = identity[None] + jnp.einsum("bmk,bnk->bmn", scaled, scaled, precision=hi)
    fro_norm = jnp.sqrt(jnp.sum(gram * gram, axis=(1, 2)))
    iterate_a = gram / fro_norm[:, None, None]
    iterate_z = jnp.broadcast_to(identity, gram.shape)
    for _ in range(ITERS):
        middle = 1.5 * identity[None] - 0.5 * jnp.einsum(
            "bij,bjk->bik", iterate_z, iterate_a, precision=hi
        )
        iterate_a = jnp.einsum("bij,bjk->bik", iterate_a, middle, precision=hi)
        iterate_z = jnp.einsum("bij,bjk->bik", middle, iterate_z, precision=hi)
    transform = iterate_z / jnp.sqrt(fro_norm)[:, None, None]
    projected = jnp.einsum("bmk,bk->bm", scaled, innovation, precision=hi)
    inner_step = jnp.einsum("bmn,bn->bm", transform, projected, precision=hi)
    mean_weights = jnp.einsum("bmn,bn->bm", transform, inner_step, precision=hi)
    weights_all = mean_weights[:, :, None] + transform
    one_hot = (assignment[:, None] == jnp.arange(MEMBERS, dtype=jnp.int32)[None, :]).astype(
        jnp.float32
    )
    ordered = jnp.einsum("bmn,nj->bmj", weights_all, one_hot, precision=hi)
    column_weights = jnp.repeat(ordered, TILE_WIDTH, axis=0)
    column_major = jnp.transpose(vertical_line_positions, (2, 0, 1))
    cell_mean = jnp.mean(column_major, axis=1)
    updated = cell_mean[:, None, :] + jnp.einsum(
        "cmj,cmx->cjx", column_weights, column_major - cell_mean[:, None, :], precision=hi
    )
    analysed = jnp.transpose(updated, (1, 2, 0))
    outgoing = analysed.reshape(group_count, local_members, slab_count, planes, own_columns)
    outgoing = jnp.transpose(outgoing, (0, 2, 1, 3, 4)).reshape(
        group_count * slab_count * local_members, planes, own_columns
    )
    result = lax.all_to_all(outgoing, ("group", "slab"), split_axis=0, concat_axis=2, tiled=True)
    return result


def shards(initial_samples, transport_ratios, assignment, obs_values, *rest):
    members, planes, columns = initial_samples.shape
    blocks = obs_values.shape[0]
    fits = (
        planes == PLANES
        and members % 8 == 0
        and blocks * TILE_WIDTH == LANES
        and lax.axis_size("slab") == 8
        and columns % LANES == 0
    )
    path = planned if fits else general
    return path(initial_samples, transport_ratios, assignment, obs_values, *rest)


def solution(mesh):
    placed = (
        P("group", "slab", None),
        P(None, "slab", None),
        P(),
        P(("group", "slab"), None),
        P(("group", "slab"), None),
        P(("group", "slab"), None),
        P(("group", "slab"), None),
        P(("group", "slab")),
    )
    return jax.shard_map(
        shards, mesh=mesh, in_specs=placed, out_specs=P("group", "slab", None), check_vma=False
    )
```

```python
import functools

import jax
import jax.numpy as jnp
from jax import lax
from jax.experimental import pallas as pl
from jax.experimental.pallas import tpu as pltpu
from jax.sharding import PartitionSpec as P


MEMBERS = 96
NZ = 64
STEPS = 6
TILE_WIDTH = 8
HC = 8
OBS = 512
ITERS = 8

LANES = 128
PLANES = 8
SPAN = 16
PACKED = 48
BATCH = 8
F32 = jnp.float32
BF16 = jnp.bfloat16
AXES = ("group", "slab")
VMEM = pl.BlockSpec(memory_space=pltpu.VMEM)
SMEM = pl.BlockSpec(memory_space=pltpu.SMEM)


def shifted(block, axis, distance):
    devices = range(lax.axis_size(axis))
    route = [((i - distance) % len(devices), i) for i in devices]
    return lax.ppermute(block, axis, route)


def lane_iota(rows=1):
    return lax.broadcasted_iota(jnp.int32, (rows, LANES), 1)


def split(x):
    high = x.astype(BF16)
    low = (x - high.astype(F32)).astype(BF16)
    return high, low


def dot(a, b, transposed=False):
    dims = (((1,), (1 if transposed else 0,)), ((), ()))
    return lax.dot_general(a, b, dims, preferred_element_type=F32)


def dot3(a, b, transposed=False):
    ah, al = a
    bh, bl = b
    return dot(ah, bh, transposed) + (dot(ah, bl, transposed) + dot(al, bh, transposed))


def tile(j):
    return pl.ds(pl.multiple_of(j * LANES, LANES), LANES)


def plane_step(src, dst, slot, rates, plane, tiles):
    lane = lane_iota()
    z_first = (lane % NZ) == 0
    upper = lane >= NZ
    octets = src.shape[1] // 8

    def at(j):
        j = (j + tiles) % tiles
        return slice(j * LANES, (j + 1) * LANES)

    for base in range(0, tiles, BATCH):
        these = range(base, min(base + BATCH, tiles))
        here = [src[slot, :, at(j)] for j in (base - 1, *these)]
        upwind = [src[slot - 1, :, at(j)] for j in these]
        below_y = [pltpu.roll(jnp.where(upper, x, y), NZ, 1) for x, y in zip(here, here[1:])]
        here = here[1:]
        one = [pltpu.roll(x, 1, 1) for x in here]
        wrapped = [pltpu.roll(x, NZ + 1, 1) for x in here]
        below_z = [jnp.where(z_first, x, y) for x, y in zip(wrapped, one)]
        for j, u, ux, uy, uz in zip(these, here, upwind, below_y, below_z):
            cx, cy, cz = (
                jnp.concatenate([rates[c, plane, :, at(j)]] * octets, axis=0) for c in range(3)
            )
            dst[slot, :, at(j)] = u - cx * (u - ux) - cy * (u - uy) - cz * (u - uz)


def fill(rates, wide):
    for c in range(3):
        for p in range(rates.shape[1]):
            wide[c, p] = jnp.broadcast_to(rates[c, p : p + 1, :], wide.shape[2:])


def first_kernel(x, ratios, skew, edge, a, b, rates):
    tiles = a.shape[2] // LANES
    fill(ratios, rates)

    def unpack(j, carry):
        a[:, :, tile(j)] = jnp.swapaxes(x[:, :, tile(j)], 0, 1)
        return carry

    lax.fori_loop(0, tiles, unpack, 0)
    edge[0] = a[PLANES - 1]

    def two_steps(kk, carry):
        k = 2 * kk + 1

        def up(i, c):
            plane_step(a, b, i, rates, i, tiles)
            return c

        def down(i, c):
            plane_step(b, a, i, rates, i, tiles)
            return c

        lax.fori_loop(k, PLANES, up, 0)
        edge[k] = b[PLANES - 1]
        lax.fori_loop(k + 1, PLANES, down, 0)

        @pl.when(k + 1 < STEPS)
        def _():
            edge[k + 1] = a[PLANES - 1]

        return carry

    lax.fori_loop(0, STEPS // 2, two_steps, 0)
    for p in range(PLANES):
        skew[p] = (a if min(p, STEPS) % 2 == 0 else b)[p]


def exchange_blocks(v):
    block = lane_iota() // SPAN
    for d in (4, 2, 1):
        high = (block // d) % 2 == 1
        out = list(v)
        for i in range(8):
            if (i // d) % 2 == 0:
                out[i] = jnp.where(high, pltpu.roll(v[i + d], SPAN * d, 1), v[i])
                out[i + d] = jnp.where(high, v[i + d], pltpu.roll(v[i], LANES - SPAN * d, 1))
        v = out
    return v


def second_kernel(half, slabs, octet, skew, halo, ratios, zh, *refs):
    keep_out, send_out, keep, send, a, b, rates, sems = refs[-8:]
    tiles = a.shape[2] // LANES
    fill(ratios, rates)
    for p in range(STEPS):
        (a if p % 2 == 0 else b)[p + 1] = skew[p]

    def two_steps(kk, carry):
        k = 2 * kk + 1

        def up(i, c):
            plane_step(a, b, i + 1, rates, i, tiles)
            return c

        def down(i, c):
            plane_step(b, a, i + 1, rates, i, tiles)
            return c

        a[0] = halo[k - 1]
        lax.fori_loop(0, k, up, 0)
        b[0] = halo[k]
        lax.fori_loop(0, k + 1, down, 0)
        return carry

    lax.fori_loop(0, STEPS // 2, two_steps, 0)

    lane = lane_iota()
    block = lane // SPAN
    members = skew.shape[1]

    def load(p, j):
        at = tile(lax.rem(j + tiles, tiles))
        return a[p + 1, :, at] if p < STEPS else skew[p, :, at]

    def moved(p, base):
        parts = [load(p, base + t) for t in range(-1, half + 1)]
        here, before = jnp.concatenate(parts[1:], axis=0), jnp.concatenate(parts[:-1], axis=0)
        return pltpu.roll(jnp.where(lane >= LANES - HC, before, here), HC, 1)

    for out, which in ((send, 1 - zh[0]), (keep, zh[0])):

        def chunk(g, carry, out=out, which=which):
            rows = [moved(p, g * slabs + which * half) for p in range(PLANES)]
            count = half * members
            after = [x[count:] for x in rows]
            last = after[0]
            for p in range(1, PLANES):
                last = jnp.where(block == p, pltpu.roll(after[p], SPAN * p, 1), last)
            groups = exchange_blocks([x[:count] for x in rows])
            for i in range(half):
                for t in range(8):
                    out[g * half + i, :, t * LANES : (t + 1) * LANES] = groups[t][
                        i * members : (i + 1) * members
                    ]
            for i in range(half - 1):
                out[g * half + i, :, 8 * LANES :] = groups[0][(i + 1) * members : (i + 2) * members]
            out[g * half + half - 1, :, 8 * LANES :] = last
            return carry

        lax.fori_loop(0, out.shape[0] // half, chunk, 0)

    at = pl.ds(octet * members, members)
    copies = [
        pltpu.make_async_copy(send, send_out.at[:, at, :], sems.at[0]),
        pltpu.make_async_copy(keep, keep_out.at[:, at, :], sems.at[1]),
    ]
    for copy in copies:
        copy.start()
    for copy in copies:
        copy.wait()


def map_kernel(half, values, errors, x, column, count, zh, keep, send):
    rows = 4 * half
    row = lax.broadcasted_iota(jnp.int32, (rows, 1), 0)
    second = (row // (2 * half)) % 2
    slab = jnp.where(second == 1, 1 - zh[0], zh[0]) * half + row % half
    is_value = (row // half) % 2 == 1
    cell = lax.broadcasted_iota(jnp.int32, (2 * LANES, OBS), 0)
    slot = lax.broadcasted_iota(jnp.int32, (1, OBS), 1)

    def body(i, carry):
        place = column[i] + TILE_WIDTH * lax.rem(i, 2)
        xs = x[i]
        lanes = (place // SPAN) * LANES + (xs % PLANES) * SPAN + place % SPAN
        hits = jnp.where(cell == lanes, 1.0, 0.0).astype(BF16)
        squared = jnp.where(slot < count[i], 1.0 / (errors[i] * (MEMBERS - 1.0)), 0.0)
        entry = jnp.where(is_value, squared * values[i], squared)
        entry = jnp.where(xs // PLANES == slab, entry, 0.0)
        one, _ = split(entry)
        two, three = split(entry - one.astype(F32))
        sums = dot(jnp.concatenate([one, two, three], axis=0), hits, True)
        total = sums[:rows] + sums[rows : 2 * rows] + sums[2 * rows :]
        keep[i] = total[: 2 * half]
        send[i] = total[2 * half :]
        return carry

    lax.fori_loop(0, values.shape[0], body, 0)


def pack(m):
    lane = lane_iota()
    top = jnp.where(lane < 96, m[64:96], pltpu.roll(m[:32], 96, 1))
    low = jnp.where(lane < 64, m[32:48], pltpu.roll(m[48:64], 64, 1))
    return top, low


def every(function, *lists):
    return [function(*x) for x in zip(*lists)]


def lower_blocks(top, low):
    lane = lane_iota()
    return jnp.concatenate(
        [
            jnp.where(lane < 32, pltpu.roll(top, 32, 1), 0.0),
            jnp.where(lane < 64, low, 0.0),
            jnp.where(lane < 64, pltpu.roll(low, 64, 1), 0.0),
            jnp.where(lane < 96, top, 0.0),
            jnp.zeros((32, LANES), F32),
        ],
        axis=0,
    )


def unpack(tops, lows):
    row = lax.broadcasted_iota(jnp.int32, (LANES, LANES), 0)
    col = lax.broadcasted_iota(jnp.int32, (LANES, LANES), 1)
    lower = every(lower_blocks, tops, lows)
    upper = [x.T for x in lower]
    return [jnp.where(row // 32 >= col // 32, x, y) for x, y in zip(lower, upper)]


def member_rows(fields, half, s, at):
    groups = fields[0].shape[0] // half
    return jnp.concatenate([f[g * half + s, :, at] for g in range(groups) for f in fields], axis=0)


def gram_kernel(half, octets, *refs):
    fields, (maps, out, anomaly, high, low, mean) = refs[:octets], refs[octets:]
    blocks = maps.shape[0]
    for s in range(half):
        for t in range(fields[0].shape[2] // LANES):
            at = slice(t * LANES, (t + 1) * LANES)
            f = member_rows(fields, half, s, at)
            average = jnp.sum(f, axis=0, keepdims=True) / MEMBERS
            f = f - average
            mean[s, :, at] = average
            anomaly[s, :, at] = f
            fh, fl = split(f)
            high[s, :MEMBERS, at] = fh
            low[s, :MEMBERS, at] = fl
            high[s, MEMBERS:, at] = jnp.zeros((LANES - MEMBERS, LANES), BF16)
            low[s, MEMBERS:, at] = jnp.zeros((LANES - MEMBERS, LANES), BF16)

    def pair(i, carry):
        at = pl.ds(pl.multiple_of(i * LANES, LANES), 2 * LANES)
        total = None
        for s in range(half):
            f = anomaly[s, :, at]
            average = mean[s, :, at]
            parts, gammas = [], []
            for e in range(2):
                omega = maps[2 * i + e, s : s + 1, :]
                value = maps[2 * i + e, half + s : half + s + 1, :]
                parts.append(f * omega)
                gammas.append(value - omega * average)
            row = lax.broadcasted_iota(jnp.int32, (8, 2 * LANES), 0)
            extra = jnp.where(row == 0, gammas[0], jnp.where(row == 1, gammas[1], 0.0))
            left = split(jnp.concatenate(parts + [extra], axis=0))
            product = dot3(left, (high[s, :, at], low[s, :, at]), True)
            total = product if total is None else total + product
        for e in range(2):
            top, bottom = pack(total[e * MEMBERS : (e + 1) * MEMBERS])
            base = pl.multiple_of((2 * i + e) * PACKED, 8)
            out[pl.ds(base, 32), :] = top
            out[pl.ds(base + 32, 16), :] = bottom
            out[pl.ds(blocks * PACKED + 2 * i + e, 1), :] = total[2 * MEMBERS + e : 2 * MEMBERS + e + 1]
        return carry

    lax.fori_loop(0, blocks // 2, pair, 0)


def solve_kernel(batch, blocks, mine, other, out, left, right, scale):
    row = lax.broadcasted_iota(jnp.int32, (LANES, LANES), 0)
    col = lax.broadcasted_iota(jnp.int32, (LANES, LANES), 1)
    identity = jnp.where((row == col) & (row < MEMBERS), 1.0, 0.0)
    steps = blocks // batch

    def each(body):
        def several(j, carry):
            at = [j * batch + e for e in range(batch)]
            for i, (a, z) in zip(at, body(at)):
                if a is not None:
                    left[i] = a
                if z is not None:
                    right[i] = z
            return carry

        lax.fori_loop(0, steps, several, 0)

    def middle(p):
        return split(1.5 * identity - 0.5 * p)

    def start(at):
        bases = [pl.multiple_of(i * PACKED, 8) for i in at]
        tops = [mine[pl.ds(x, 32), :] + other[pl.ds(x, 32), :] for x in bases]
        lows = [mine[pl.ds(x + 32, 16), :] + other[pl.ds(x + 32, 16), :] for x in bases]
        grams = [identity + x for x in unpack(tops, lows)]
        sums = [jnp.sum(g * g, axis=0, keepdims=True) for g in grams]
        sums = [jnp.sum(x, axis=1, keepdims=True) for x in sums]
        roots = [lax.rsqrt(x) for x in sums]
        for i, x in zip(at, roots):
            scale[i] = jnp.broadcast_to(x, (8, LANES))
        return [(g * x, None) for g, x in zip(grams, roots)]

    def second(at):
        a = [left[i] for i in at]
        m = [1.5 * identity - 0.5 * x for x in a]
        return zip(every(dot3, every(split, a), every(split, m)), m)

    def iterate(at):
        a = [split(left[i]) for i in at]
        z = [split(right[i]) for i in at]
        m = every(middle, every(dot3, z, a))
        return zip(every(dot3, a, m), every(dot3, m, z))

    def last(at):
        a = [split(left[i]) for i in at]
        z = [split(right[i]) for i in at]
        m = every(middle, every(dot3, z, a))
        return [(None, x) for x in every(dot3, m, z)]

    def finish(at):
        rows = [pl.ds(blocks * PACKED + i, 1) for i in at]
        done = [right[i, :MEMBERS] * jnp.sqrt(scale[i, :1]) for i in at]
        vectors = [mine[x, :] + other[x, :] for x in rows]
        inner = [jnp.sum(t * x, axis=1, keepdims=True) for t, x in zip(done, vectors)]
        means = [jnp.sum(t * x, axis=0, keepdims=True) for t, x in zip(done, inner)]
        packs = every(pack, done)
        for i, x, m, (top, low) in zip(at, rows, means, packs):
            base = pl.multiple_of(i * PACKED, 8)
            out[pl.ds(base, 32), :] = top
            out[pl.ds(base + 32, 16), :] = low
            out[x, :] = m
        return []

    def loop(k, carry):
        each(iterate)
        return carry

    each(start)
    each(second)
    lax.fori_loop(1, ITERS - 1, loop, 0)
    each(last)
    each(finish)


def apply_kernel(half, blocks, octets, *refs):
    fields, (weights, assignment, out, result, planar) = refs[:octets], refs[octets:]
    members = out.shape[1]
    lane = lane_iota()
    first = (lane % SPAN) < TILE_WIDTH

    def pair(i, carry):
        bases = [pl.multiple_of((2 * i + e) * PACKED, 8) for e in range(2)]
        tops = [weights[pl.ds(x, 32), :] for x in bases]
        sides = unpack(tops, [weights[pl.ds(x + 32, 16), :] for x in bases])
        rows_at = [pl.ds(blocks * PACKED + 2 * i + e, 1) for e in range(2)]
        sides = [t[:MEMBERS] + weights[x, :] for t, x in zip(sides, rows_at)]
        left = split(jnp.concatenate(sides, axis=1))
        filler = jnp.zeros((LANES - MEMBERS, LANES), F32)
        for s in range(half):

            rows = functools.partial(member_rows, fields, half, s)
            x = jnp.where(
                first,
                pltpu.roll(rows(tile(i)), LANES - TILE_WIDTH, 1),
                pltpu.roll(rows(tile(i + 1)), TILE_WIDTH, 1),
            )
            average = jnp.sum(x, axis=0, keepdims=True) / MEMBERS
            x = x - average
            right = jnp.concatenate(
                [jnp.where(first, x, 0.0), filler, jnp.where(first, 0.0, x), filler], axis=0
            )
            result[s, i] = average + dot3(left, split(right))
        return carry

    lax.fori_loop(0, blocks // 2, pair, 0)
    for s in range(half):
        for r in range(MEMBERS // 8):
            at = slice(8 * r, 8 * r + 8)
            planes = exchange_blocks([result[s, i, at, :] for i in range(8)])
            for p in range(PLANES):
                planar[p * MEMBERS + 8 * r : p * MEMBERS + 8 * r + 8, :] = planes[p]

        def hand(n, carry, s=s):
            member = assignment[n]
            g, m = lax.div(member, members), lax.rem(member, members)
            out[g * half + s, m] = planar[pl.ds(n, PLANES, stride=MEMBERS), :]
            return carry

        lax.fori_loop(0, MEMBERS, hand, 0, unroll=8)


def join_kernel(half, mine, other, zh, out):
    for source, which in ((mine, zh[0]), (other, 1 - zh[0])):
        for s in range(half):
            out[:, :, tile(which * half + s)] = source[s]


def call(kernel, outs, scratch, *args, specs=None, cost=None, room=20, grid=()):
    shapes = [jax.ShapeDtypeStruct(s, F32) for s in outs]
    return pl.pallas_call(
        kernel,
        out_shape=shapes if len(shapes) > 1 else shapes[0],
        grid=grid,
        in_specs=specs or [VMEM] * len(args),
        out_specs=[VMEM] * len(shapes) if len(shapes) > 1 else VMEM,
        scratch_shapes=scratch,
        compiler_params=pltpu.CompilerParams(vmem_limit_bytes=room * 1024 * 1024),
        cost_estimate=cost,
    )(*args)


def work(flops, moved):
    return pl.CostEstimate(flops=flops, bytes_accessed=moved, transcendentals=0)


def planned(
    initial_samples,
    transport_ratios,
    assignment,
    obs_values,
    obs_error,
    sensor_easting_offset,
    obs_column,
    obs_count,
):
    members, planes, columns = initial_samples.shape
    slabs = lax.axis_size("slab")
    groups = lax.axis_size("group")
    half = slabs // 2
    peers = groups * half
    blocks = obs_values.shape[0]
    width = blocks // 2 * LANES + LANES
    zh = (lax.axis_index("slab") // half).astype(jnp.int32).reshape(1)
    teams = [
        [g * slabs + h * half + i for g in range(groups) for i in range(half)] for h in range(2)
    ]

    def spread(x):
        return lax.all_to_all(
            x, AXES, split_axis=0, concat_axis=0, tiled=True, axis_index_groups=teams
        )

    def partner(x):
        return shifted(x, "slab", half)

    octets = members // 8
    map_shape = (blocks, 2 * half, 2 * LANES)
    whole = (planes, 8, columns)
    wide = [pltpu.VMEM((3, planes, 8, columns), F32)]
    firsts, halos = [], []
    for c in range(octets):
        skew, edge = call(
            first_kernel,
            [whole, (STEPS, 8, columns)],
            [pltpu.VMEM(whole, F32)] * 2 + wide,
            initial_samples,
            transport_ratios,
            specs=[pl.BlockSpec((8, planes, columns), lambda i, c=c: (c, 0, 0)), VMEM],
            cost=work(10**7, 4 * 10**6),
            grid=(1,),
        )
        firsts.append(skew)
        halos.append(shifted(edge, "slab", 1))
    map_keep, map_send = call(
        functools.partial(map_kernel, half),
        [map_shape, map_shape],
        [],
        *(x[:, None] for x in (obs_values, obs_error, sensor_easting_offset, obs_column)),
        obs_count,
        zh,
        specs=[VMEM] * 4 + [SMEM] * 2,
        cost=work(10**8, 10**6),
    )
    map_recv = partner(map_send)
    payload = jax.ShapeDtypeStruct((peers, members, width), F32)
    part = pltpu.VMEM((peers, 8, width), F32)
    anywhere = pl.BlockSpec(memory_space=pl.ANY)
    held = []
    for c in range(octets):
        held = pl.pallas_call(
            functools.partial(second_kernel, half, slabs, c),
            out_shape=[payload, payload],
            in_specs=[VMEM] * 3 + [SMEM] + [anywhere] * len(held),
            out_specs=[anywhere] * 2,
            scratch_shapes=[part, part]
            + [pltpu.VMEM((STEPS + 1, 8, columns), F32)] * 2
            + wide
            + [pltpu.SemaphoreType.DMA((2,))],
            input_output_aliases={4: 0, 5: 1} if held else {},
            compiler_params=pltpu.CompilerParams(vmem_limit_bytes=20 * 1024 * 1024),
            cost_estimate=work(10**7, 4 * 10**6),
        )(firsts[c], halos[c], transport_ratios, zh, *held)
    fields_send = [spread(held[1])]
    fields_keep = [spread(held[0])]
    packed = (blocks * PACKED + blocks, LANES)

    def gram(fields, maps):
        return call(
            functools.partial(gram_kernel, half, 1),
            [packed],
            [
                pltpu.VMEM((half, MEMBERS, width), F32),
                pltpu.VMEM((half, LANES, width), BF16),
                pltpu.VMEM((half, LANES, width), BF16),
                pltpu.VMEM((half, 1, width), F32),
            ],
            *fields,
            maps,
            cost=work(10**9, 4 * 10**6),
        )

    def apply(fields, weights):
        return call(
            functools.partial(apply_kernel, half, blocks, 1),
            [(peers, members, planes, LANES)],
            [
                pltpu.VMEM((half, blocks // 2, MEMBERS, LANES), F32),
                pltpu.VMEM((PLANES * MEMBERS, LANES), F32),
            ],
            *fields,
            weights,
            assignment,
            specs=[VMEM] * 2 + [SMEM],
            cost=work(10**9, 4 * 10**6),
        )

    gram_send = gram(fields_send, map_recv)
    gram_other = partner(gram_send)
    gram_mine = gram(fields_keep, map_keep)
    weights = call(
        functools.partial(solve_kernel, blocks, blocks),
        [packed],
        [pltpu.VMEM((blocks, LANES, LANES), F32)] * 2 + [pltpu.VMEM((blocks, 8, LANES), F32)],
        gram_mine,
        gram_other,
        cost=work(10**9, 10**6),
    )
    weights_other = partner(weights)
    applied = apply(fields_keep, weights)
    result_mine = spread(applied)
    result_other = spread(apply(fields_send, weights_other))
    part = pl.BlockSpec((half, members, planes, LANES), lambda g: (g, 0, 0, 0))
    return pl.pallas_call(
        functools.partial(join_kernel, half),
        out_shape=jax.ShapeDtypeStruct((members, planes, columns), F32),
        grid=(groups,),
        in_specs=[part, part, SMEM],
        out_specs=pl.BlockSpec((members, planes, slabs * LANES), lambda g: (0, 0, g)),
    )(result_mine, result_other, zh)


def padded(x, sides, width):
    for axis, dim in sides:
        size, length = (lax.axis_size(axis), x.shape[dim])
        up = [(i, (i + 1) % size) for i in range(size)]
        down = [(j, i) for i, j in up]
        last = lax.slice_in_dim(x, length - width, length, axis=dim)
        first = lax.slice_in_dim(x, 0, width, axis=dim)
        before = lax.ppermute(last, axis, up)
        after = lax.ppermute(first, axis, down)
        x = jnp.concatenate([before, x, after], axis=dim)
    return x


def advance(sample_state, upwind, rates):
    z_position = jnp.arange(sample_state.shape[2]) % NZ
    below_y = jnp.roll(sample_state, NZ, axis=2)
    below_z = jnp.where(
        z_position == 0, jnp.roll(sample_state, 1 - NZ, axis=2), jnp.roll(sample_state, 1, axis=2)
    )
    return (
        sample_state
        - rates[0] * (sample_state - upwind)
        - rates[1] * (sample_state - below_y)
        - rates[2] * (sample_state - below_z)
    )


def general(
    initial_samples,
    transport_ratios,
    assignment,
    obs_values,
    obs_error,
    sensor_easting_offset,
    obs_column,
    obs_count,
):
    hi = lax.Precision.HIGHEST
    local_members, planes, total_columns = initial_samples.shape
    group_count = lax.axis_size("group")
    slab_count = lax.axis_size("slab")
    own_columns = total_columns // (group_count * slab_count)
    state = initial_samples
    for _ in range(STEPS):
        edge_plane = shifted(state[:, planes - 1 :], "slab", 1)
        upwind = jnp.concatenate([edge_plane, state[:, : planes - 1]], axis=1)
        state = advance(state, upwind, transport_ratios)
    pieces = lax.all_to_all(state, ("group", "slab"), split_axis=2, concat_axis=0, tiled=True)
    pieces = pieces.reshape(group_count, slab_count, local_members, planes, own_columns)
    vertical_line_positions = jnp.transpose(pieces, (0, 2, 1, 3, 4)).reshape(
        MEMBERS, slab_count * planes, own_columns
    )
    grid_x = vertical_line_positions.shape[1]
    own_blocks = obs_values.shape[0]
    block_start = (TILE_WIDTH * jnp.arange(own_blocks, dtype=jnp.int32))[:, None]
    edge_blocks = (HC + TILE_WIDTH - 1) // TILE_WIDTH
    window_col = block_start - HC + obs_column
    requests = jnp.stack([sensor_easting_offset, obs_column])
    asked = padded(requests, ((("group", "slab"), 1),), edge_blocks)
    left_asked = asked[:, :edge_blocks]
    right_asked = asked[:, edge_blocks + own_blocks :]
    edge_index = jnp.arange(edge_blocks, dtype=jnp.int32)[:, None]
    left_cols = (
        TILE_WIDTH * (own_blocks - edge_blocks + edge_index) - HC + left_asked[1] - own_columns
    )
    right_cols = TILE_WIDTH * edge_index - HC + right_asked[1] + own_columns
    serve_level = jnp.concatenate([left_asked[0], right_asked[0]], axis=0)
    serve_cols = jnp.clip(jnp.concatenate([left_cols, right_cols], axis=0), 0, own_columns - 1)
    flattened = vertical_line_positions.reshape(MEMBERS, grid_x * own_columns)
    serve_pos = (serve_level * own_columns + serve_cols).reshape(-1)
    served = jnp.take(flattened, serve_pos, axis=1).reshape(MEMBERS, 2 * edge_blocks, OBS)
    answered = padded(served, ((("group", "slab"), 1),), edge_blocks)
    from_left = answered[:, :edge_blocks]
    from_right = answered[:, 3 * edge_blocks :]
    filler = jnp.zeros((MEMBERS, own_blocks - edge_blocks, OBS), jnp.float32)
    left_full = jnp.concatenate([from_left, filler], axis=1)
    right_full = jnp.concatenate([filler, from_right], axis=1)
    local_pos = (
        sensor_easting_offset * own_columns + jnp.clip(window_col, 0, own_columns - 1)
    ).reshape(-1)
    local_vals = jnp.take(flattened, local_pos, axis=1).reshape(MEMBERS, own_blocks, OBS)
    modelled_readings = jnp.where(
        window_col[None] < 0,
        left_full,
        jnp.where(window_col[None] >= own_columns, right_full, local_vals),
    )
    slots = jnp.arange(OBS, dtype=jnp.int32)[None, :]
    pred_mean = jnp.mean(modelled_readings, axis=0)
    weight = jnp.where(slots < obs_count[:, None], 1.0 / jnp.sqrt(obs_error * (MEMBERS - 1.0)), 0.0)
    scaled = jnp.transpose((modelled_readings - pred_mean[None]) * weight[None], (1, 0, 2))
    innovation = (obs_values - pred_mean) * weight
    identity = jnp.eye(MEMBERS, dtype=jnp.float32)
    gram = identity[None] + jnp.einsum("bmk,bnk->bmn", scaled, scaled, precision=hi)
    fro_norm = jnp.sqrt(jnp.sum(gram * gram, axis=(1, 2)))
    iterate_a = gram / fro_norm[:, None, None]
    iterate_z = jnp.broadcast_to(identity, gram.shape)
    for _ in range(ITERS):
        middle = 1.5 * identity[None] - 0.5 * jnp.einsum(
            "bij,bjk->bik", iterate_z, iterate_a, precision=hi
        )
        iterate_a = jnp.einsum("bij,bjk->bik", iterate_a, middle, precision=hi)
        iterate_z = jnp.einsum("bij,bjk->bik", middle, iterate_z, precision=hi)
    transform = iterate_z / jnp.sqrt(fro_norm)[:, None, None]
    projected = jnp.einsum("bmk,bk->bm", scaled, innovation, precision=hi)
    inner_step = jnp.einsum("bmn,bn->bm", transform, projected, precision=hi)
    mean_weights = jnp.einsum("bmn,bn->bm", transform, inner_step, precision=hi)
    weights_all = mean_weights[:, :, None] + transform
    one_hot = (assignment[:, None] == jnp.arange(MEMBERS, dtype=jnp.int32)[None, :]).astype(
        jnp.float32
    )
    ordered = jnp.einsum("bmn,nj->bmj", weights_all, one_hot, precision=hi)
    column_weights = jnp.repeat(ordered, TILE_WIDTH, axis=0)
    column_major = jnp.transpose(vertical_line_positions, (2, 0, 1))
    cell_mean = jnp.mean(column_major, axis=1)
    updated = cell_mean[:, None, :] + jnp.einsum(
        "cmj,cmx->cjx", column_weights, column_major - cell_mean[:, None, :], precision=hi
    )
    analysed = jnp.transpose(updated, (1, 2, 0))
    outgoing = analysed.reshape(group_count, local_members, slab_count, planes, own_columns)
    outgoing = jnp.transpose(outgoing, (0, 2, 1, 3, 4)).reshape(
        group_count * slab_count * local_members, planes, own_columns
    )
    result = lax.all_to_all(outgoing, ("group", "slab"), split_axis=0, concat_axis=2, tiled=True)
    return result


def shards(initial_samples, transport_ratios, assignment, obs_values, *rest):
    members, planes, columns = initial_samples.shape
    blocks = obs_values.shape[0]
    fits = (
        planes == PLANES
        and members % 8 == 0
        and blocks * TILE_WIDTH == LANES
        and lax.axis_size("slab") == 8
        and columns % LANES == 0
    )
    path = planned if fits else general
    return path(initial_samples, transport_ratios, assignment, obs_values, *rest)


def solution(mesh):
    placed = (
        P("group", "slab", None),
        P(None, "slab", None),
        P(),
        P(("group", "slab"), None),
        P(("group", "slab"), None),
        P(("group", "slab"), None),
        P(("group", "slab"), None),
        P(("group", "slab")),
    )
    return jax.shard_map(
        shards, mesh=mesh, in_specs=placed, out_specs=P("group", "slab", None), check_vma=False
    )
```
